32 devices in a mesh: node: 16 (over z, x, core), local: 2 (over y).
Axes of the slice: x: 2, y: 2, z: 4, core: 2. Of those that a mesh axis runs over, the one named last changes fastest.
Arguments:
- tokens: bfloat16 [512, 2560], P(('node', 'local')), may hold values from -6 to 6
- expert_ids: int32 [512, 6], P(('node', 'local')), may hold values from 0 to 31, as said below
- gate_probs: bfloat16 [512, 6], P(('node', 'local')), may hold values from 0.25 to 1
- failed: int32 [1], replicated, may hold values from 0 to 15
- backup: int32 [16], replicated, may hold values from 0 to 15, as said below
- expert_gate: bfloat16 [32, 2560, 1280], P(('node', 'local')), may hold values from -0.125 to 0.125
- expert_up: bfloat16 [32, 2560, 1280], P(('node', 'local')), may hold values from -0.125 to 0.125
- expert_down: bfloat16 [32, 1280, 2560], P(('node', 'local')), may hold values from -0.15625 to 0.15625
- shared_gate: bfloat16 [2560, 1536], P('node', 'local'), may hold values from -0.125 to 0.125
- shared_up: bfloat16 [2560, 1536], P('node', 'local'), may hold values from -0.125 to 0.125
- shared_down: bfloat16 [1536, 2560], P('local', 'node'), may hold values from -0.15625 to 0.15625
Outputs:
- mixed: bfloat16 [512, 2560], P(('node', 'local'))
The draws below stay inside these ranges and needn't reach their ends.
Inputs may be any that keep to these rules, and one draw needn't show every extreme that they name: `expert_ids`: A token's six experts lie on exactly four distinct nodes, node m holding experts 2 m and 2 m + 1: columns 0 and 1 name both experts of one node, columns 2 and 3 both experts of a second, column 4 one expert of a third and column 5 one expert of a fourth. Among the 16 tokens of one device (aligned blocks of rows), at most 4 name any one node, and some node is named by exactly 4 of them. backup[m] differs from m.
All inputs are finite; a program needn't handle non-finite values.
Results may differ from the reference program's by a relative error of at most 0.01.
Values may be sent and summed in bfloat16 or wider, within the bound.
No kernel may reach another device: no remote copies, remote signals or barrier semaphores. Data moves between devices by JAX's collectives and lax.ppermute only.
A program may use at most 64 MiB of HBM per device.

```python
import jax
import jax.numpy as jnp
from jax import lax

D = 2560
H = 1280
HS = 1536
EXP_NODE = 2
TOPK = 6
TOK_DEV = 16
EXPERTS = 32
HSPLIT = 1
HSLICE = 1280
HS_DEV = 768
LANE = 4
CAP = 4
TOKENS = 512
N_NODE = 16
N_LOCAL = 2


def draw_expert_ids(key, part):
    block_total = TOKENS // TOK_DEV
    node_total = EXPERTS // EXP_NODE

    def one_block(block_index):
        block_key = jax.random.fold_in(key, block_index)
        ordering = jax.random.permutation(jax.random.fold_in(block_key, 7), node_total)
        columns = []
        for lane_index in range(4):
            shuffled = jax.random.permutation(jax.random.fold_in(block_key, lane_index + 11), TOK_DEV)
            picked = lane_index * LANE + shuffled % LANE
            chosen_node = jnp.take(ordering, picked)
            if lane_index < 2:
                columns.append(EXP_NODE * chosen_node)
                columns.append(EXP_NODE * chosen_node + 1)
            else:
                side = jax.random.randint(jax.random.fold_in(block_key, lane_index + 31), (TOK_DEV,), 0, EXP_NODE)
                columns.append(EXP_NODE * chosen_node + side)
        return jnp.stack(columns, axis=1).astype(jnp.int32)
    blocks = jax.vmap(one_block)(jnp.arange(block_total, dtype=jnp.int32))
    return blocks.reshape(TOKENS, TOPK).astype(jnp.int32)


def draw_backup(key, part):
    node_total = EXPERTS // EXP_NODE
    offsets = jax.random.randint(key, (node_total,), 1, node_total)
    return ((jnp.arange(node_total, dtype=jnp.int32) + offsets) % node_total).astype(jnp.int32)


def block_scale(key, dims, shards, smallest, high):
    def one(position, shards_of):
        steps = jax.random.uniform(jax.random.fold_in(jax.random.fold_in(key, 6), position), (shards_of,), jnp.float32, smallest / len(shards), high / len(shards))
        return jnp.repeat(jnp.exp(steps), dims[position] // shards_of).reshape((-1,) + (1,) * (len(dims) - position - 1))

    gain = one(*shards[0])
    for cut in shards[1:]:
        gain = gain * one(*cut)
    return gain


def gaussian(stream_key, extent, width, bound, cuts=(), kind=jnp.bfloat16):
    entries = jax.random.normal(stream_key, extent, jnp.float32) * width
    if len(cuts) > 0:
        entries = block_scale(stream_key, extent, cuts, -0.22, 0.18) * entries
    return jnp.clip(entries, min=-bound, max=bound).astype(kind)


def setup_inputs(seed: int = 0) -> dict:
    seeds = jax.random.split(jax.random.key(seed), 12)
    return {
        "tokens": gaussian(seeds[0], (TOKENS, D), 1.0, 6.0, ((0, 32),)),
        "expert_ids": draw_expert_ids(jax.random.fold_in(seeds[11], 71), 0),
        "gate_probs": jnp.clip(0.25 + 0.75 * jax.random.uniform(seeds[2], (TOKENS, TOPK), jnp.float32) ** block_scale(seeds[2], (TOKENS, TOPK), ((0, 32),), -0.2, 0.2), 0.25, 1.0).astype(jnp.bfloat16),
        "failed": jax.random.randint(seeds[3], (1,), 0, N_NODE).astype(jnp.int32),
        "backup": draw_backup(jax.random.fold_in(seeds[11], 71), 0),
        "expert_gate": gaussian(seeds[5], (EXPERTS * HSPLIT, D, HSLICE), D ** -0.5, 0.125, ((0, 32),)),
        "expert_up": gaussian(seeds[6], (EXPERTS * HSPLIT, D, HSLICE), D ** -0.5, 0.125, ((0, 32),)),
        "expert_down": gaussian(seeds[7], (EXPERTS * HSPLIT, HSLICE, D), H ** -0.5, 0.15625, ((0, 32),)),
        "shared_gate": gaussian(seeds[8], (D, HS), D ** -0.5, 0.125, ((0, 16), (1, 2))),
        "shared_up": gaussian(seeds[9], (D, HS), D ** -0.5, 0.125, ((0, 16), (1, 2))),
        "shared_down": gaussian(seeds[10], (HS, D), HS ** -0.5, 0.15625, ((0, 2), (1, 16))),
    }


def row_layout(expert_ids, gate_probs):
    probs = gate_probs.astype(jnp.float32)
    node_of = jnp.stack([expert_ids[:, 0], expert_ids[:, 2], expert_ids[:, 4], expert_ids[:, 5]], axis=1) // EXP_NODE
    third_low = (expert_ids[:, 4] % EXP_NODE == 0).astype(jnp.float32)
    fourth_low = (expert_ids[:, 5] % EXP_NODE == 0).astype(jnp.float32)
    first_pair = jnp.stack([probs[:, 0], probs[:, 1]], axis=1)
    second_pair = jnp.stack([probs[:, 2], probs[:, 3]], axis=1)
    third_pair = jnp.stack([probs[:, 4] * third_low, probs[:, 4] * (1.0 - third_low)], axis=1)
    fourth_pair = jnp.stack([probs[:, 5] * fourth_low, probs[:, 5] * (1.0 - fourth_low)], axis=1)
    pair_probs = jnp.stack([first_pair, second_pair, third_pair, fourth_pair], axis=1)
    return node_of.astype(jnp.int32), pair_probs


def reference(tokens, expert_ids, gate_probs, failed, backup, expert_gate, expert_up, expert_down, shared_gate, shared_up, shared_down):
    failed_node = failed[0]
    helper = jnp.sum(jnp.where(jnp.arange(N_NODE, dtype=jnp.int32) == failed_node, backup, 0)).astype(jnp.int32)
    node_of, pair_all = row_layout(expert_ids, gate_probs)
    node_flat = node_of.reshape(-1)
    pair_probs = pair_all.reshape(TOKENS * 4, 2)
    row_limit = N_NODE * N_LOCAL * CAP

    def per_node(total, node_index):
        chosen_flat = node_flat == node_index
        selected = jnp.nonzero(chosen_flat, size=row_limit, fill_value=0)[0].astype(jnp.int32)
        live = (jnp.arange(row_limit, dtype=jnp.int32) < jnp.sum(chosen_flat.astype(jnp.int32))).astype(jnp.float32)
        token_rows = (selected // 4).astype(jnp.int32)
        rows_in = tokens[token_rows]
        weights_pair = pair_probs[selected] * live[:, None]
        host = jnp.where(node_index == failed_node, helper, node_index).astype(jnp.int32)
        first_index = (host * N_LOCAL).astype(jnp.int32)
        gate_slices = lax.dynamic_slice_in_dim(expert_gate, first_index, N_LOCAL, 0)
        up_slices = lax.dynamic_slice_in_dim(expert_up, first_index, N_LOCAL, 0)
        down_slices = lax.dynamic_slice_in_dim(expert_down, first_index, N_LOCAL, 0)
        summed = jnp.zeros((row_limit, D), jnp.float32)
        for slice_index in range(N_LOCAL):
            weight_col = weights_pair[:, slice_index // HSPLIT]
            first = jnp.dot(rows_in, gate_slices[slice_index], preferred_element_type=jnp.float32)
            second = jnp.dot(rows_in, up_slices[slice_index], preferred_element_type=jnp.float32)
            hidden = (weight_col[:, None] * jax.nn.silu(first) * second).astype(jnp.bfloat16)
            part = jnp.dot(hidden, down_slices[slice_index], preferred_element_type=jnp.float32).astype(jnp.bfloat16)
            summed = summed + lax.optimization_barrier(part).astype(jnp.float32)
        return total.at[token_rows].add(summed), None

    routed, _ = lax.scan(per_node, jnp.zeros((TOKENS, D), jnp.float32), jnp.arange(N_NODE, dtype=jnp.int32))
    shared_first = jnp.dot(tokens, shared_gate, preferred_element_type=jnp.float32)
    shared_second = jnp.dot(tokens, shared_up, preferred_element_type=jnp.float32)
    shared_hidden = (jax.nn.silu(shared_first) * shared_second).astype(jnp.bfloat16)
    shared = jnp.zeros((TOKENS, D), jnp.float32)
    for slice_index in range(HS // HS_DEV):
        lower = slice_index * HS_DEV
        part = jnp.dot(shared_hidden[:, lower:lower + HS_DEV], shared_down[lower:lower + HS_DEV, :], preferred_element_type=jnp.float32).astype(jnp.bfloat16)
        shared = shared + lax.optimization_barrier(part).astype(jnp.float32)
    return (shared + routed).astype(jnp.bfloat16)
```

```python
import functools

import jax
import jax.numpy as jnp
from jax import lax
from jax.experimental import pallas as pl
from jax.experimental.pallas import tpu as pltpu
from jax.sharding import PartitionSpec as P

H = 1280
EXP_NODE = 2
AXES = ("node", "local")
LANES = 128
BF16 = jnp.bfloat16
F32 = jnp.float32


def up_kernel(count, pick_ref, *refs):
    blocks = refs[:count]
    gate_ref, upw_ref, hidden_ref, rows_ref, prob_ref = refs[count:]
    width = rows_ref.shape[1]
    per = blocks[0].shape[0]

    @pl.when(pl.program_id(0) == 0)
    def _():
        lane = lax.broadcasted_iota(jnp.int32, (LANES, LANES), 0)
        pick = jnp.where((lane == pick_ref[0]) | (lane == pick_ref[1]), 1.0, 0.0).astype(BF16)
        for k in range(count):
            spot = pl.ds(k * per, per)
            rows_ref[spot, :] = blocks[k][:, :width]
            prob_ref[spot, :] = jnp.dot(
                blocks[k][:, width:], pick, preferred_element_type=F32
            )

    first = jnp.dot(rows_ref[...], gate_ref[0], preferred_element_type=F32)
    second = jnp.dot(rows_ref[...], upw_ref[0], preferred_element_type=F32)
    prob = prob_ref[:, :1]
    hidden_ref[...] = (prob * (first * jax.nn.sigmoid(first)) * second).astype(BF16)


def up_call(pick, blocks, expert_gate, expert_up, tile):
    width, hidden = expert_gate.shape[1:]
    rows = sum(b.shape[0] for b in blocks)
    weight = pl.BlockSpec((1, width, tile), lambda i, s: (0, 0, i))
    return pl.pallas_call(
        functools.partial(up_kernel, len(blocks)),
        grid_spec=pltpu.PrefetchScalarGridSpec(
            num_scalar_prefetch=1,
            grid=(hidden // tile,),
            in_specs=[pl.BlockSpec(b.shape, lambda i, s: (0, 0)) for b in blocks] + [weight, weight],
            out_specs=pl.BlockSpec((rows, tile), lambda i, s: (0, i)),
            scratch_shapes=[pltpu.VMEM((rows, width), BF16), pltpu.VMEM((rows, LANES), F32)],
        ),
        out_shape=jax.ShapeDtypeStruct((rows, hidden), BF16),
        compiler_params=pltpu.CompilerParams(vmem_limit_bytes=40 << 20),
        cost_estimate=pl.CostEstimate(
            flops=4 * rows * width * hidden,
            bytes_accessed=4 * width * hidden + 2 * rows * (width + hidden),
            transcendentals=rows * hidden,
        ),
        name="expert_up",
    )(pick, *blocks, expert_gate, expert_up)


def down_kernel(count, *refs):
    blocks = refs[:count]
    hidden_ref, down_ref, shared_in_ref, shared_out_ref, own_ref, other_ref, rows_ref, shared_ref = refs[count:]
    width = rows_ref.shape[1]
    per = blocks[0].shape[0]
    units = shared_out_ref.shape[0]
    half = own_ref.shape[0]

    @pl.when(pl.program_id(0) == 0)
    def _():
        for k in range(count):
            rows_ref[pl.ds(k * per, per), :] = blocks[k][:, :width]
        both = jnp.dot(rows_ref[...], shared_in_ref[...], preferred_element_type=F32)
        first = both[:, : LANES // 2]
        second = both[:, LANES // 2 :]
        shared_ref[...] = ((first * jax.nn.sigmoid(first)) * second).astype(BF16)

    total = jnp.dot(hidden_ref[...], down_ref[0], preferred_element_type=F32)
    total = total + jnp.dot(
        shared_ref[:, :units], shared_out_ref[...], preferred_element_type=F32
    )
    own_ref[...] = total[:half].astype(BF16)
    other_ref[...] = total[half:].astype(BF16)


def down_call(blocks, hidden_rows, expert_down, shared_in, shared_out, tile):
    hidden, width = expert_down.shape[1:]
    rows = hidden_rows.shape[0]
    units = shared_out.shape[0]
    half = rows // 2
    out = jax.ShapeDtypeStruct((half, width), BF16)
    out_spec = pl.BlockSpec((half, tile), lambda i: (0, i))
    return pl.pallas_call(
        functools.partial(down_kernel, len(blocks)),
        grid=(width // tile,),
        in_specs=[pl.BlockSpec(b.shape, lambda i: (0, 0)) for b in blocks]
        + [
            pl.BlockSpec((rows, hidden), lambda i: (0, 0)),
            pl.BlockSpec((1, hidden, tile), lambda i: (0, 0, i)),
            pl.BlockSpec((width, LANES), lambda i: (0, 0)),
            pl.BlockSpec((units, tile), lambda i: (0, i)),
        ],
        out_specs=[out_spec, out_spec],
        out_shape=[out, out],
        scratch_shapes=[pltpu.VMEM((rows, width), BF16), pltpu.VMEM((rows, LANES // 2), BF16)],
        compiler_params=pltpu.CompilerParams(vmem_limit_bytes=40 << 20),
        cost_estimate=pl.CostEstimate(
            flops=2 * rows * width * (hidden + 2 * LANES),
            bytes_accessed=2 * width * hidden + 2 * rows * (2 * width + hidden),
            transcendentals=rows * LANES,
        ),
        name="expert_down",
    )(*blocks, hidden_rows, expert_down, shared_in, shared_out)


def dense_body(
    tokens, expert_ids, gate_probs, failed, backup,
    expert_gate, expert_up, expert_down, shared_gate, shared_up, shared_down,
):
    tok_dev, width = tokens.shape
    node_count = lax.axis_size("node")
    local_count = lax.axis_size("local")
    me, my_local = lax.axis_index("node"), lax.axis_index("local")
    total = node_count * local_count
    y, core, x = 1, local_count, 2 * local_count
    z = [4 * local_count * k for k in range(node_count // 4)]
    quad = [x, y, x | y]

    def swap(value, bits):
        return lax.ppermute(value, AXES, [(i, i ^ bits) for i in range(total)])

    part = shared_gate.shape[1] // node_count
    split_gate = shared_gate.reshape(-1, node_count, part).transpose(1, 0, 2)
    split_up = shared_up.reshape(-1, node_count, part).transpose(1, 0, 2)
    pad = ((0, 0), (0, 0), (0, LANES // 2 - part))
    both = jnp.concatenate([jnp.pad(split_gate, pad), jnp.pad(split_up, pad)], axis=2)
    shared_in = lax.all_to_all(both, "node", split_axis=0, concat_axis=0, tiled=True)
    shared_in = shared_in.reshape(width, LANES)
    split_down = shared_down.reshape(node_count, part, -1)
    shared_out = lax.all_to_all(split_down, "node", split_axis=0, concat_axis=0, tiled=True)
    shared_out = shared_out.transpose(1, 0, 2).reshape(part, width)

    lanes = jnp.arange(LANES, dtype=jnp.int32)
    weights = jnp.sum(
        jnp.where(expert_ids[:, :, None] == lanes, gate_probs[:, :, None].astype(F32), 0.0), axis=1
    ).astype(BF16)
    mine = jnp.concatenate([tokens, weights], axis=1)

    failed_node = failed[0]
    helper = jnp.sum(jnp.where(jnp.arange(node_count, dtype=jnp.int32) == failed_node, backup, 0))
    pick = jnp.stack([
        jnp.where(me == failed_node, -1, 2 * me + my_local),
        jnp.where(me == helper, 2 * failed_node + my_local, -1),
    ]).astype(jnp.int32)

    column = jnp.concatenate([mine] + [swap(mine, k) for k in z[1:]], axis=0)
    far = [swap(column, k) for k in quad]
    column_other = swap(column, core)
    far_other = [swap(b, core) for b in far]
    near_blocks = [column, column_other]
    far_blocks = far + far_other

    near_hidden = up_call(pick, near_blocks, expert_gate, expert_up, 256)
    far_hidden = up_call(pick, far_blocks, expert_gate, expert_up, 256)
    far_own, far_give = down_call(far_blocks, far_hidden, expert_down, shared_in, shared_out, 512)
    near_own, near_give = down_call(near_blocks, near_hidden, expert_down, shared_in, shared_out, 512)

    rows = column.shape[0]
    far_got = swap(far_give, core)
    near_got = swap(near_give, core)
    sums = (far_own.astype(F32) + far_got.astype(F32)).astype(BF16)
    arrived = [swap(sums[k * rows : (k + 1) * rows], b) for k, b in enumerate(quad)]
    plane = near_own.astype(F32) + near_got.astype(F32)
    for a in arrived:
        plane = plane + a.astype(F32)
    plane16 = plane.astype(BF16)
    result = plane[:tok_dev]
    for k in range(1, len(z)):
        result = result + swap(plane16[k * tok_dev : (k + 1) * tok_dev], z[k]).astype(F32)
    return result.astype(BF16)


def row_layout(expert_ids, gate_probs):
    probs = gate_probs.astype(jnp.float32)
    node_of = (
        jnp.stack([expert_ids[:, 0], expert_ids[:, 2], expert_ids[:, 4], expert_ids[:, 5]], axis=1)
        // EXP_NODE
    )
    third_low = (expert_ids[:, 4] % EXP_NODE == 0).astype(jnp.float32)
    fourth_low = (expert_ids[:, 5] % EXP_NODE == 0).astype(jnp.float32)
    first_pair = jnp.stack([probs[:, 0], probs[:, 1]], axis=1)
    second_pair = jnp.stack([probs[:, 2], probs[:, 3]], axis=1)
    third_pair = jnp.stack([probs[:, 4] * third_low, probs[:, 4] * (1.0 - third_low)], axis=1)
    fourth_pair = jnp.stack([probs[:, 5] * fourth_low, probs[:, 5] * (1.0 - fourth_low)], axis=1)
    pair_probs = jnp.stack([first_pair, second_pair, third_pair, fourth_pair], axis=1)
    return (node_of, pair_probs)


def body(
    tokens,
    expert_ids,
    gate_probs,
    failed,
    backup,
    expert_gate,
    expert_up,
    expert_down,
    shared_gate,
    shared_up,
    shared_down,
):
    tok_dev, width = tokens.shape
    node_count = lax.axis_size("node")
    local_count = lax.axis_size("local")
    my_local = lax.axis_index("local")
    lane_width = node_count // 4
    capacity = -(-tok_dev // lane_width)
    split_count = H // expert_gate.shape[2]
    failed_node = failed[0]
    node_range = jnp.arange(node_count, dtype=jnp.int32)
    helper = jnp.sum(jnp.where(node_range == failed_node, backup, 0))
    node_tokens = lax.all_gather(tokens, "local", axis=0, tiled=True)
    shared_first = jnp.dot(
        node_tokens,
        lax.all_gather(shared_gate, "node", axis=0, tiled=True),
        preferred_element_type=jnp.float32,
    )
    shared_second = jnp.dot(
        node_tokens,
        lax.all_gather(shared_up, "node", axis=0, tiled=True),
        preferred_element_type=jnp.float32,
    )
    shared_hidden = (jax.nn.silu(shared_first) * shared_second).astype(jnp.bfloat16)
    shared_terms = jnp.dot(
        shared_hidden,
        lax.all_gather(shared_down, "node", axis=1, tiled=True),
        preferred_element_type=jnp.float32,
    ).astype(jnp.bfloat16)
    shared_terms = lax.optimization_barrier(shared_terms)
    node_of, pair_probs = row_layout(expert_ids, gate_probs)
    member = (node_of[:, :, None] == node_range).astype(jnp.float32)
    earlier = (jnp.arange(tok_dev)[:, None] > jnp.arange(tok_dev)[None, :]).astype(jnp.float32)
    before = jnp.dot(earlier, jnp.sum(member, axis=1), precision=lax.Precision.HIGHEST)
    arrival = jnp.sum(member * before[:, None, :], axis=2).astype(jnp.int32)
    on_failed = node_of == failed_node
    weight_gate = expert_gate[0]
    weight_up = expert_up[0]
    weight_down = expert_down[0]
    slot_count = 2 * capacity
    target = jnp.where(on_failed, helper, node_of)
    place_slot = arrival + jnp.where(on_failed, capacity, 0)
    row_total = node_count * slot_count
    position = target * slot_count + place_slot
    slot_range = jnp.arange(row_total, dtype=jnp.int32)
    placement_map = (position[:, :, None] == slot_range).astype(jnp.float32)
    assign = jnp.sum(placement_map, axis=1)
    send_rows = lax.dot_general(
        assign.astype(jnp.bfloat16),
        tokens,
        (((0,), (0,)), ((), ())),
        preferred_element_type=jnp.float32,
    ).astype(jnp.bfloat16)
    send_probs = jnp.einsum(
        "tjp,tjc->pc", placement_map, pair_probs, precision=lax.Precision.HIGHEST
    ).astype(jnp.bfloat16)
    arrived_rows, arrived_probs = (
        lax.all_to_all(
            send_rows.reshape(node_count, slot_count, width),
            "node",
            split_axis=0,
            concat_axis=0,
            tiled=True,
        ),
        lax.all_to_all(
            send_probs.reshape(node_count, slot_count, 2),
            "node",
            split_axis=0,
            concat_axis=0,
            tiled=True,
        ),
    )
    all_rows, all_probs = (
        lax.all_gather(arrived_rows.reshape(1, row_total, width), "local", axis=0, tiled=True),
        lax.all_gather(arrived_probs.reshape(1, row_total, 2), "local", axis=0, tiled=True),
    )
    flat_rows = all_rows.reshape(local_count * row_total, width)
    flat_probs = all_probs.reshape(local_count * row_total, 2)
    expert_side = my_local // split_count
    chosen = jnp.where(expert_side == 0, flat_probs[:, 0], flat_probs[:, 1]).astype(jnp.float32)
    first = jnp.dot(flat_rows, weight_gate, preferred_element_type=jnp.float32)
    second = jnp.dot(flat_rows, weight_up, preferred_element_type=jnp.float32)
    routed_hidden = (chosen[:, None] * jax.nn.silu(first) * second).astype(jnp.bfloat16)
    routed_terms = jnp.dot(routed_hidden, weight_down, preferred_element_type=jnp.float32).astype(
        jnp.bfloat16
    )
    routed_terms = routed_terms.reshape(local_count, row_total, width)
    returned = lax.all_to_all(routed_terms, "local", split_axis=0, concat_axis=0, tiled=True)
    node_sums = jnp.sum(returned.astype(jnp.float32), axis=0)
    shared_mine = lax.psum_scatter(
        shared_terms.astype(jnp.float32).astype(jnp.bfloat16),
        "local",
        scatter_dimension=0,
        tiled=True,
    ).astype(jnp.float32)
    results_back = lax.all_to_all(
        node_sums.reshape(node_count, slot_count, width).astype(jnp.bfloat16),
        "node",
        split_axis=0,
        concat_axis=0,
        tiled=True,
    ).astype(jnp.float32)
    routed_mine = jnp.dot(
        assign, results_back.reshape(row_total, width), precision=lax.Precision.HIGHEST
    )
    return (shared_mine + routed_mine).astype(jnp.bfloat16)


def solution(mesh):
    dense = mesh.shape["node"] == 16 and mesh.shape["local"] == 2
    return jax.shard_map(
        dense_body if dense else body,
        mesh=mesh,
        in_specs=(
            P(("node", "local"), None),
            P(("node", "local"), None),
            P(("node", "local"), None),
            P(),
            P(),
            P(("node", "local"), None, None),
            P(("node", "local"), None, None),
            P(("node", "local"), None, None),
            P("node", "local"),
            P("node", "local"),
            P("local", "node"),
        ),
        out_specs=P(("node", "local"), None),
        check_vma=False,
    )
```
